32 devices in a mesh: fs: 4 (over z), sp: 8 (over y, x, core).
Axes of the slice: x: 2, y: 2, z: 4, core: 2. Of those that a mesh axis runs over, the one named last changes fastest.
Arguments:
- tokens: bfloat16 [4, 2048, 2048], P('fs', 'sp'), may hold values from -6 to 6
- positions: int32 [4, 2048], P('fs'), may hold values from 0 to 4095
- query_weight: bfloat16 [2048, 2048], P('fs', 'sp'), may hold values from -0.125 to 0.125
- key_weight: bfloat16 [2048, 2048], P('fs', 'sp'), may hold values from -0.125 to 0.125
- value_weight: bfloat16 [2048, 2048], P('fs', 'sp'), may hold values from -0.125 to 0.125
- output_weight: bfloat16 [2048, 2048], P('sp', 'fs'), may hold values from -0.125 to 0.125
- gate_weight: bfloat16 [2048, 8192], P('fs', 'sp'), may hold values from -0.125 to 0.125
- up_weight: bfloat16 [2048, 8192], P('fs', 'sp'), may hold values from -0.125 to 0.125
- down_weight: bfloat16 [8192, 2048], P('sp', 'fs'), may hold values from -0.0625 to 0.0625
- query_gain: bfloat16 [2048], replicated, may hold values from 0 to 9
- key_gain: bfloat16 [2048], replicated, may hold values from 0 to 9
- attention_gain: bfloat16 [2048], replicated, may hold values from 0.5 to 1.5
- feedforward_gain: bfloat16 [2048], replicated, may hold values from 0.5 to 1.5
- out_grad: bfloat16 [4, 2048, 2048], P('fs', 'sp'), may hold values from -6 to 6
Outputs:
- block_output: bfloat16 [4, 2048, 2048], P('fs', 'sp')
- tokens_grad: float32 [4, 2048, 2048], P('fs', 'sp')
- query_weight_grad: float32 [2048, 2048], P('fs', 'sp')
- key_weight_grad: float32 [2048, 2048], P('fs', 'sp')
- value_weight_grad: float32 [2048, 2048], P('fs', 'sp')
- output_weight_grad: float32 [2048, 2048], P('sp', 'fs')
- gate_weight_grad: float32 [2048, 8192], P('fs', 'sp')
- up_weight_grad: float32 [2048, 8192], P('fs', 'sp')
- down_weight_grad: float32 [8192, 2048], P('sp', 'fs')
- query_gain_grad: float32 [2048], replicated
- key_gain_grad: float32 [2048], replicated
- attention_gain_grad: float32 [2048], replicated
- feedforward_gain_grad: float32 [2048], replicated
The draws below stay inside these ranges and needn't reach their ends.
All inputs are finite; a program needn't handle non-finite values.
Results may differ from the reference program's by a relative error of at most 0.02.
The reference program's roundings to bfloat16 on the way count: a program that leaves them out, or rounds other values in their place, can miss the bound.
Values may be sent and summed in bfloat16 or wider, within the bound.
No kernel may reach another device: no remote copies, remote signals or barrier semaphores. Data moves between devices by JAX's collectives and lax.ppermute only.
A program may use at most 256 MiB of HBM per device.

```python
import jax
import jax.numpy as jnp
import numpy as np
from jax import lax

D = 2048
H = 16
HD = 128
FF = 8192
LEN = 2048
SEQ_ALL = 4
QB = 512


def head_gain(key):
    noise = jax.random.normal(jax.random.fold_in(key, 1), (H, HD), jnp.float32)
    gains = jnp.clip(1.0 + 0.1 * noise, 0.7, 1.3)
    return gains.reshape(H * HD).astype(jnp.bfloat16)


def draw_query_gain(key, part):
    return head_gain(jax.random.fold_in(key, 11))


def draw_key_gain(key, part):
    return head_gain(jax.random.fold_in(key, 12))


def touch_ends(drawn, own_key, least, largest):
    spot = [jax.random.randint(jax.random.fold_in(own_key, axis), (), 0, length) for axis, length in enumerate(drawn.shape)]
    widest = drawn.shape.index(max(drawn.shape))
    next_to = spot[:widest] + [(spot[widest] + 1) % drawn.shape[widest]] + spot[widest + 1:]
    return drawn.at[tuple(spot)].set(least).at[tuple(next_to)].set(largest)


def shard_levels(stream_key, shape, cuts, least, top_value):
    level, own = 1.0, jax.random.fold_in(stream_key, 6)
    for position, parts in cuts:
        draws = jnp.exp(jax.random.uniform(jax.random.fold_in(own, position), (parts,), jnp.float32, least / len(cuts), top_value / len(cuts)))
        level = level * jnp.repeat(draws, shape[position] // parts).reshape([-1 if axis == position else 1 for axis in range(len(shape))])
    return level


def bell_draw(key, dims, scale, bound, shards=(), held_as=jnp.bfloat16):
    entries = scale * jax.random.normal(key, dims, jnp.float32)
    if shards:
        entries = entries * shard_levels(key, dims, shards, -0.22, 0.18)
    return jnp.clip(entries, -bound, bound).astype(held_as)


def setup_inputs(seed: int = 0) -> dict:
    key_of = jax.random.split(jax.random.key(seed), 15)
    tokens = bell_draw(key_of[0], (SEQ_ALL, LEN, D), 1.0, 6.0, ((0, 4), (1, 8)))
    positions = touch_ends(jax.random.randint(key_of[1], (SEQ_ALL, LEN), 0, 2 * LEN), jax.random.fold_in(key_of[1], 1), 0, (2 * LEN) - 1).astype(jnp.int32)
    query_weight = bell_draw(key_of[2], (D, D), D ** -0.5, 0.125, ((0, 4), (1, 8)))
    key_weight = bell_draw(key_of[3], (D, D), D ** -0.5, 0.125, ((0, 4), (1, 8)))
    value_weight = bell_draw(key_of[4], (D, D), D ** -0.5, 0.125, ((0, 4), (1, 8)))
    output_weight = bell_draw(key_of[5], (D, D), D ** -0.5, 0.125, ((0, 8), (1, 4)))
    gate_weight = bell_draw(key_of[6], (D, FF), D ** -0.5, 0.125, ((0, 4), (1, 8)))
    up_weight = bell_draw(key_of[7], (D, FF), D ** -0.5, 0.125, ((0, 4), (1, 8)))
    down_weight = bell_draw(key_of[8], (FF, D), FF ** -0.5, 0.0625, ((0, 8), (1, 4)))
    query_gain = draw_query_gain(jax.random.fold_in(key_of[14], 71), 0)
    key_gain = draw_key_gain(jax.random.fold_in(key_of[14], 71), 0)
    attention_gain = jnp.clip(1.0 + 0.1 * jax.random.normal(key_of[11], (D,), jnp.float32), 0.5, 1.5).astype(jnp.bfloat16)
    feedforward_gain = jnp.clip(1.0 + 0.1 * jax.random.normal(key_of[12], (D,), jnp.float32), 0.5, 1.5).astype(jnp.bfloat16)
    out_grad = bell_draw(key_of[13], (SEQ_ALL, LEN, D), 1.0, 6.0, ((0, 4), (1, 8)))
    return dict(tokens=tokens, positions=positions, query_weight=query_weight, key_weight=key_weight, value_weight=value_weight, output_weight=output_weight, gate_weight=gate_weight, up_weight=up_weight, down_weight=down_weight, query_gain=query_gain, key_gain=key_gain, attention_gain=attention_gain, feedforward_gain=feedforward_gain, out_grad=out_grad)


EPS = 1e-06
THETA = 500000.0
HIGH = lax.Precision.HIGHEST

@jax.custom_vjp
def low(v):
    return lax.optimization_barrier(v.astype(jnp.bfloat16)).astype(jnp.float32)

@jax.custom_vjp
def low_back(v):
    return v

def low_keep(v):
    return (low(v), None)

def low_pass(kept, grad):
    return (grad,)

def back_keep(v):
    return (v, None)

def back_low(kept, grad):
    return (low(grad),)
low.defvjp(low_keep, low_pass)
low_back.defvjp(back_keep, back_low)

def matmul(left, right):
    return jnp.dot(left, right, precision=HIGH, preferred_element_type=jnp.float32)

def rms_scale(field, gain):
    inverse = lax.rsqrt(lax.optimization_barrier(jnp.mean(field * field, axis=-1, keepdims=True)) + EPS)
    return field * inverse * gain

def rotary_tables(positions, width):
    half = width // 2
    table = jnp.asarray(np.power(THETA, -np.arange(half) * 2.0 / width).astype(np.float32))
    angles = positions.astype(jnp.float32)[:, None] * table[None, :]
    return (jnp.cos(angles)[:, None, :], jnp.sin(angles)[:, None, :])

def rotate(field, cosine, sine):
    half = field.shape[-1] // 2
    first_half = field[..., :half]
    second_half = field[..., half:]
    return jnp.concatenate([first_half * cosine - second_half * sine, second_half * cosine + first_half * sine], axis=-1)

def attention_block(first_row, query_all, key_all, value_all):
    query_rows = lax.dynamic_slice_in_dim(query_all, first_row, QB, 0)
    scores = jnp.einsum('qhd,khd->hqk', query_rows, key_all, precision=HIGH) * HD ** (-0.5)
    scores = low_back(scores)
    query_index = first_row + jnp.arange(QB, dtype=jnp.int32)
    key_index = jnp.arange(LEN, dtype=jnp.int32)
    allowed = key_index[None, :] <= query_index[:, None]
    scores = jnp.where(allowed[None], scores, -1e+30)
    row_max = lax.optimization_barrier(jnp.max(scores, axis=-1, keepdims=True))
    expo = jnp.exp(scores - row_max)
    softmax_rows = expo / lax.optimization_barrier(jnp.sum(expo, axis=-1, keepdims=True))
    return jnp.einsum('hqk,khd->qhd', low(softmax_rows), value_all, precision=HIGH)

def layer(params, inputs, positions):
    query_weight, key_weight, value_weight, output_weight, gate_weight, up_weight, down_weight, query_gain, key_gain, attention_gain, feedforward_gain = params
    query_proj = low_back(matmul(inputs, query_weight))
    key_proj = low_back(matmul(inputs, key_weight))
    value_rows = low_back(low(matmul(inputs, value_weight))).reshape(LEN, H, HD)
    cosine, sine = rotary_tables(positions, HD)
    query_rot = low_back(low(rotate(rms_scale(query_proj, query_gain).reshape(LEN, H, HD), cosine, sine)))
    key_rot = low_back(low(rotate(rms_scale(key_proj, key_gain).reshape(LEN, H, HD), cosine, sine)))
    first_rows = jnp.arange(LEN // QB, dtype=jnp.int32) * QB
    block_fn = jax.checkpoint(lambda first_row: attention_block(first_row, query_rot, key_rot, value_rows))
    context = lax.map(block_fn, first_rows).reshape(LEN, D)
    context = low_back(low(context))
    attn_out = low_back(matmul(context, output_weight))
    hidden = inputs + rms_scale(attn_out, attention_gain)
    mixed_in = low(hidden)
    gate_proj = low_back(matmul(mixed_in, gate_weight))
    up_proj = low_back(matmul(mixed_in, up_weight))
    active = low(jax.nn.silu(gate_proj) * up_proj)
    mlp_out = low_back(matmul(active, down_weight))
    return hidden + rms_scale(mlp_out, feedforward_gain)

def reference(tokens, positions, query_weight, key_weight, value_weight, output_weight, gate_weight, up_weight, down_weight, query_gain, key_gain, attention_gain, feedforward_gain, out_grad):
    params = tuple((weight.astype(jnp.float32) for weight in (query_weight, key_weight, value_weight, output_weight, gate_weight, up_weight, down_weight, query_gain, key_gain, attention_gain, feedforward_gain)))
    inputs = tokens.astype(jnp.float32)
    layer_fn = jax.checkpoint(layer)

    def forward(params, inputs):

        def advance(carry, element):
            sequence, position_row = element
            return (carry, layer_fn(params, sequence, position_row))
        unused, outputs = lax.scan(advance, jnp.zeros((), jnp.float32), (inputs, positions))
        return outputs
    outputs, pullback = jax.vjp(forward, params, inputs)
    param_grads, input_grad = pullback(out_grad.astype(jnp.float32))
    return (outputs.astype(jnp.bfloat16), input_grad, param_grads[0], param_grads[1], param_grads[2], param_grads[3], param_grads[4], param_grads[5], param_grads[6], param_grads[7], param_grads[8], param_grads[9], param_grads[10])
```

```python
import jax
import jax.numpy as jnp
import numpy as np
from jax import lax
from jax.experimental import pallas as pl
from jax.experimental.pallas import tpu as pltpu
from jax.sharding import PartitionSpec as P

HD = 128
EPS = 1e-06
THETA = 500000.0
SCALE = HD ** (-0.5)
F32 = jnp.float32
BF16 = jnp.bfloat16


def product(left, right):
    return jnp.dot(left, right, preferred_element_type=F32)


def left_product(left, right):
    return lax.dot_general(left, right, (((0,), (0,)), ((), ())), preferred_element_type=F32)


def right_product(left, right):
    return lax.dot_general(left, right, (((1,), (1,)), ((), ())), preferred_element_type=F32)


def swap(value, axis, bit):
    count = lax.axis_size(axis)
    return lax.ppermute(value, axis, [(i, i ^ bit) for i in range(count)])


def chip_bits():
    count = lax.axis_size("sp")
    return [1 << b for b in range(1, count.bit_length() - 1)]


def gather_chips(value):
    bits = chip_bits()
    if len(bits) == 2:
        half = value.shape[0] // 2
        low = swap(value, "sp", bits[0])
        high = swap(value, "sp", bits[1])
        both = jnp.concatenate(
            [swap(high[:half], "sp", bits[0]), swap(low[half:], "sp", bits[1])], axis=0
        )
        return [value, low, high, both]
    slots = [value]
    for bit in bits:
        slots = slots + [swap(slot, "sp", bit) for slot in slots]
    return slots


def gather_rows(value):
    own = gather_chips(value)
    other = [swap(slot, "sp", 1) for slot in own]
    return jnp.concatenate(own + other, axis=0)


def halve(slots, bits):
    current = dict(enumerate(slots))
    for bit in bits:
        index = bit >> 1
        sent = sorted(mask for mask in current if mask & index)
        moved = swap(jnp.stack([current[mask] for mask in sent]).astype(BF16), "sp", bit)
        for place, mask in enumerate(sent):
            current[mask ^ index] = current[mask ^ index] + moved[place].astype(F32)
            del current[mask]
    return current[0]


def scatter_rows(own_half, other_half):
    bits = chip_bits()
    chips = 1 << len(bits)
    total = own_half + swap(other_half, "sp", 1).astype(F32)
    rows = total.shape[0] // chips
    half = rows // 2
    first = [total[k * rows : k * rows + half] for k in range(chips)]
    second = [total[k * rows + half : (k + 1) * rows] for k in range(chips)]
    return jnp.concatenate([halve(first, bits), halve(second, bits[::-1])], axis=0)


def sum_rows(value):
    count = lax.axis_size("sp")
    chips = count // 2
    lead, rows = value.shape
    value = value.reshape(lead, 2, chips, rows // count)
    bit = 1
    while bit < count:
        moved = swap(value, "sp", bit)
        if bit == 1:
            moved = moved[:, ::-1]
        else:
            order = [k ^ (bit >> 1) for k in range(chips)]
            moved = jnp.stack([moved[:, :, k] for k in order], axis=2)
        value = value + moved
        bit *= 2
    return value.reshape(lead, rows)


def sum_all(value):
    for axis in ("sp", "fs"):
        bit = 1
        while bit < lax.axis_size(axis):
            value = value + swap(value, axis, bit)
            bit *= 2
    return value


def slot_start(block, chip, core, chips, rows):
    return pl.multiple_of(((((block & 1) ^ core) * chips) + ((block >> 1) ^ chip)) * rows, rows)


def read_pair(ref, index, chip, core, chips, rows):
    low = ref[pl.ds(slot_start(2 * index, chip, core, chips, rows), rows), :]
    high = ref[pl.ds(slot_start(2 * index + 1, chip, core, chips, rows), rows), :]
    return jnp.concatenate([low, high], axis=0)


def write_pair(ref, index, chip, core, chips, rows, value):
    ref[pl.ds(slot_start(2 * index, chip, core, chips, rows), rows), :] = value[:rows]
    ref[pl.ds(slot_start(2 * index + 1, chip, core, chips, rows), rows), :] = value[rows:]


def add_pair(ref, index, chip, core, chips, rows, value):
    low = pl.ds(slot_start(2 * index, chip, core, chips, rows), rows)
    high = pl.ds(slot_start(2 * index + 1, chip, core, chips, rows), rows)
    ref[low, :] = ref[low, :] + value[:rows]
    ref[high, :] = ref[high, :] + value[rows:]


def causal(size):
    key = lax.broadcasted_iota(jnp.int32, (size, size), 0)
    query = lax.broadcasted_iota(jnp.int32, (size, size), 1)
    return key <= query


def attention_forward(place, query, key, value):
    total_rows, columns = query.shape
    heads = columns // HD
    count = lax.axis_size("sp")
    chips = count // 2
    rows = total_rows // count
    size = 2 * rows

    def kernel(place_ref, q_ref, k_ref, v_ref, own_ref, abs_ref, lse_ref, score_ref):
        chip, core = place_ref[0], place_ref[1]
        index = pl.program_id(1)
        at = (chip, core, chips, rows)
        q = read_pair(q_ref, index, *at)

        def score(t):
            return right_product(read_pair(k_ref, t, *at), q) * SCALE

        def first(t, top):
            scores = score(t)
            score_ref[t] = scores
            return jnp.maximum(top, jnp.max(scores, axis=0, keepdims=True))

        last = jnp.where(causal(size), score(index), -1e30)
        score_ref[index] = last
        top = lax.fori_loop(0, index, first, jnp.max(last, axis=0, keepdims=True))

        def second(t, total):
            expo = jnp.exp(score_ref[t] - top)
            score_ref[t] = expo
            return total + jnp.sum(expo, axis=0, keepdims=True)

        total = lax.fori_loop(0, index + 1, second, jnp.zeros((1, size), F32))
        inverse = 1.0 / total

        def third(t, acc):
            weights = (score_ref[t] * inverse).astype(BF16)
            return acc + left_product(read_pair(v_ref, t, *at), weights)

        acc = lax.fori_loop(0, index + 1, third, jnp.zeros((HD, size), F32))
        context = acc.T.astype(BF16)
        abs_ref[...] = context
        write_pair(own_ref, index, *at, context)
        lse_ref[0] = top + jnp.log(total)

    full = pl.BlockSpec((total_rows, HD), lambda h, i, s: (0, h))
    chunk = pl.BlockSpec((size, HD), lambda h, i, s: (i, h))
    return pl.pallas_call(
        kernel,
        grid_spec=pltpu.PrefetchScalarGridSpec(
            num_scalar_prefetch=1,
            grid=(heads, chips),
            in_specs=[full, full, full],
            out_specs=[full, chunk, pl.BlockSpec((1, 1, size), lambda h, i, s: (h, 0, i))],
            scratch_shapes=[pltpu.VMEM((chips, size, size), F32)],
        ),
        out_shape=[
            jax.ShapeDtypeStruct((total_rows, columns), BF16),
            jax.ShapeDtypeStruct((total_rows, columns), BF16),
            jax.ShapeDtypeStruct((heads, 1, total_rows), F32),
        ],
        compiler_params=pltpu.CompilerParams(dimension_semantics=("arbitrary", "arbitrary")),
        name="attention_forward",
    )(place, query, key, value)


def attention_backward(place, query, key, value, context_grad, lse):
    total_rows, columns = query.shape
    heads = columns // HD
    count = lax.axis_size("sp")
    chips = count // 2
    rows = total_rows // count
    size = 2 * rows

    def kernel(
        place_ref, q_ref, k_ref, v_ref, g_ref, lse_ref, dq_ref, dk_ref, dv_ref,
        prob_ref, grad_ref, key_acc, value_acc,
    ):
        chip, core = place_ref[0], place_ref[1]
        index = pl.program_id(1)
        at = (chip, core, chips, rows)
        q = read_pair(q_ref, index, *at)
        g = g_ref[...]
        row_lse = lse_ref[0]

        @pl.when(index == 0)
        def _():
            key_acc[...] = jnp.zeros_like(key_acc)
            value_acc[...] = jnp.zeros_like(value_acc)

        def first(t, inner, masked):
            scores = right_product(read_pair(k_ref, t, *at), q) * SCALE
            if masked:
                scores = jnp.where(causal(size), scores, -1e30)
            prob = jnp.exp(scores - row_lse)
            prob_grad = right_product(read_pair(v_ref, t, *at), g)
            prob_ref[t] = prob
            grad_ref[t] = prob_grad
            add_pair(value_acc, t, *at, product(prob.astype(BF16), g))
            return inner + jnp.sum(prob * prob_grad, axis=0, keepdims=True)

        inner = first(index, jnp.zeros((1, size), F32), True)
        inner = lax.fori_loop(0, index, lambda t, acc: first(t, acc, False), inner)

        def second(t, acc):
            score_grad = (prob_ref[t] * (grad_ref[t] - inner)).astype(BF16)
            add_pair(key_acc, t, *at, product(score_grad, q))
            return acc + left_product(read_pair(k_ref, t, *at), score_grad)

        acc = lax.fori_loop(0, index + 1, second, jnp.zeros((HD, size), F32))
        write_pair(dq_ref, index, *at, (acc.T * SCALE).astype(BF16))

        @pl.when(index == chips - 1)
        def _():
            dk_ref[...] = (key_acc[...] * SCALE).astype(BF16)
            dv_ref[...] = value_acc[...].astype(BF16)

    full = pl.BlockSpec((total_rows, HD), lambda h, i, s: (0, h))
    chunk = pl.BlockSpec((size, HD), lambda h, i, s: (i, h))
    return pl.pallas_call(
        kernel,
        grid_spec=pltpu.PrefetchScalarGridSpec(
            num_scalar_prefetch=1,
            grid=(heads, chips),
            in_specs=[
                full, full, full, chunk, pl.BlockSpec((1, 1, size), lambda h, i, s: (h, 0, i))
            ],
            out_specs=[full, full, full],
            scratch_shapes=[
                pltpu.VMEM((chips, size, size), F32),
                pltpu.VMEM((chips, size, size), F32),
                pltpu.VMEM((total_rows, HD), F32),
                pltpu.VMEM((total_rows, HD), F32),
            ],
        ),
        out_shape=[jax.ShapeDtypeStruct((total_rows, columns), BF16)] * 3,
        compiler_params=pltpu.CompilerParams(dimension_semantics=("arbitrary", "arbitrary")),
        name="attention_backward",
    )(place, query, key, value, context_grad, lse)


def rope_forward(query, key, query_inverse, key_inverse, query_scale, key_scale, cosine, sine):
    total_rows, columns = query.shape
    size = min(512, total_rows)

    def kernel(q_ref, k_ref, qi_ref, ki_ref, qs_ref, ks_ref, c_ref, s_ref, qo_ref, ko_ref):
        cos, sin = c_ref[...], s_ref[...]
        for src, inv, gain, out in (
            (q_ref, qi_ref, qs_ref, qo_ref), (k_ref, ki_ref, ks_ref, ko_ref)
        ):
            for h in range(columns // HD):
                span = slice(h * HD, (h + 1) * HD)
                normed = src[:, span] * inv[...] * gain[:, span]
                turned = pltpu.roll(normed, HD // 2, 1)
                out[:, span] = (normed * cos + turned * sin).astype(BF16)

    block = pl.BlockSpec((size, columns), lambda i: (i, 0))
    thin = pl.BlockSpec((size, 1), lambda i: (i, 0))
    gain = pl.BlockSpec((1, columns), lambda i: (0, 0))
    table = pl.BlockSpec((size, HD), lambda i: (i, 0))
    return pl.pallas_call(
        kernel,
        grid=(total_rows // size,),
        in_specs=[block, block, thin, thin, gain, gain, table, table],
        out_specs=[block, block],
        out_shape=[jax.ShapeDtypeStruct((total_rows, columns), BF16)] * 2,
        name="rope_forward",
    )(query, key, query_inverse, key_inverse, query_scale, key_scale, cosine, sine)


def rope_backward(
    query_grad, key_grad, query, key, query_inverse, key_inverse, query_scale, key_scale,
    cosine, sine,
):
    total_rows, columns = query.shape
    size = min(512, total_rows)

    def kernel(
        dq_ref, dk_ref, q_ref, k_ref, qi_ref, ki_ref, qs_ref, ks_ref, c_ref, s_ref,
        qo_ref, ko_ref, qn_ref, kn_ref, qg_ref, kg_ref,
    ):
        cos, sin = c_ref[...], s_ref[...]
        start = pl.program_id(0) == 0
        for grad, src, inv, gain, out, inner_ref, gain_ref in (
            (dq_ref, q_ref, qi_ref, qs_ref, qo_ref, qn_ref, qg_ref),
            (dk_ref, k_ref, ki_ref, ks_ref, ko_ref, kn_ref, kg_ref),
        ):
            inner = jnp.zeros((size, HD), F32)
            for h in range(columns // HD):
                span = slice(h * HD, (h + 1) * HD)
                value = grad[:, span].astype(F32)
                normed = value * cos - pltpu.roll(value, HD // 2, 1) * sin
                out[:, span] = normed
                field = src[:, span]
                inner = inner + normed * gain[:, span] * field
                part = jnp.sum(normed * field * inv[...], axis=0, keepdims=True)
                gain_ref[:, span] = jnp.where(start, part, gain_ref[:, span] + part)
            inner_ref[...] = jnp.sum(inner, axis=1, keepdims=True)

    block = pl.BlockSpec((size, columns), lambda i: (i, 0))
    thin = pl.BlockSpec((size, 1), lambda i: (i, 0))
    gain = pl.BlockSpec((1, columns), lambda i: (0, 0))
    table = pl.BlockSpec((size, HD), lambda i: (i, 0))
    return pl.pallas_call(
        kernel,
        grid=(total_rows // size,),
        in_specs=[block, block, block, block, thin, thin, gain, gain, table, table],
        out_specs=[block, block, thin, thin, gain, gain],
        out_shape=[
            jax.ShapeDtypeStruct((total_rows, columns), F32),
            jax.ShapeDtypeStruct((total_rows, columns), F32),
            jax.ShapeDtypeStruct((total_rows, 1), F32),
            jax.ShapeDtypeStruct((total_rows, 1), F32),
            jax.ShapeDtypeStruct((1, columns), F32),
            jax.ShapeDtypeStruct((1, columns), F32),
        ],
        name="rope_backward",
    )(
        query_grad, key_grad, query, key, query_inverse, key_inverse, query_scale, key_scale,
        cosine, sine,
    )


def norm_apply(field, gain):
    inverse = lax.rsqrt(jnp.mean(field * field, axis=-1, keepdims=True) + EPS)
    return (field * inverse * gain, inverse)


def norm_back(incoming, field, inverse, gain):
    scaled = incoming * gain
    inner = jnp.mean(scaled * field, axis=-1, keepdims=True)
    field_grad = inverse * scaled - field * inverse * inverse * inverse * inner
    gain_part = jnp.sum(incoming * field * inverse, axis=0)
    return (field_grad, gain_part)


def rotary_tables(positions):
    half = HD // 2
    table = jnp.asarray(np.power(THETA, -np.arange(half) * 2.0 / HD).astype(np.float32))
    angles = positions.astype(F32)[:, None] * table[None, :]
    cosine, sine = jnp.cos(angles), jnp.sin(angles)
    return (
        jnp.concatenate([cosine, cosine], axis=1),
        jnp.concatenate([-sine, sine], axis=1),
    )


def body(
    tokens,
    positions,
    query_weight,
    key_weight,
    value_weight,
    output_weight,
    gate_weight,
    up_weight,
    down_weight,
    query_gain,
    key_gain,
    attention_gain,
    feedforward_gain,
    out_grad,
):
    seq_count, local_len, width = tokens.shape
    assert seq_count == 1
    count = lax.axis_size("sp")
    chips = count // 2
    rows = local_len * count
    half = rows // 2
    columns = query_weight.shape[1]
    me = lax.axis_index("sp")
    place = jnp.stack([me >> 1, me & 1]).astype(jnp.int32)
    column_start = me * columns

    def gather_weight(weight, axis):
        return lax.all_gather(weight, "fs", axis=axis, tiled=True)

    query_cols = gather_weight(query_weight, 0)
    key_cols = gather_weight(key_weight, 0)
    value_cols = gather_weight(value_weight, 0)
    output_part = gather_weight(output_weight, 1)
    gate_cols = gather_weight(gate_weight, 0)
    up_cols = gather_weight(up_weight, 0)
    down_part = gather_weight(down_weight, 1)

    query_scale = lax.dynamic_slice_in_dim(query_gain.astype(F32), column_start, columns)[None]
    key_scale = lax.dynamic_slice_in_dim(key_gain.astype(F32), column_start, columns)[None]
    attention_scale = attention_gain.astype(F32)
    feedforward_scale = feedforward_gain.astype(F32)

    slots = np.concatenate([np.arange(chips) * 2, np.arange(chips) * 2 + 1])
    block_of = me ^ jnp.asarray(slots, jnp.int32)
    own_positions = jnp.take(positions.reshape(count, local_len), block_of, axis=0).reshape(rows)
    cosine, sine = rotary_tables(own_positions)

    inputs_low = tokens.reshape(local_len, width)
    inputs_all = gather_rows(inputs_low)
    query_proj = product(inputs_all, query_cols)
    key_proj = product(inputs_all, key_cols)
    squares = sum_rows(
        jnp.stack([jnp.sum(query_proj * query_proj, axis=1), jnp.sum(key_proj * key_proj, axis=1)])
    )
    value_low = product(inputs_all, value_cols).astype(BF16)
    inverses = lax.rsqrt(squares / width + EPS)
    query_inverse = inverses[0][:, None]
    key_inverse = inverses[1][:, None]
    query_rot, key_rot = rope_forward(
        query_proj, key_proj, query_inverse, key_inverse, query_scale, key_scale, cosine, sine
    )
    context_own, context_abs, log_total = attention_forward(place, query_rot, key_rot, value_low)
    context_local = lax.all_to_all(context_abs, "sp", split_axis=0, concat_axis=1, tiled=True)

    output_slots = gather_rows(output_part)
    output_full = jnp.take(
        output_slots.reshape(count, columns, width), inverse_slots(me, count), axis=0
    ).reshape(width, width)
    attn_out = product(context_local, output_full)
    inputs_local = inputs_low.astype(F32)
    attn_normed, attn_inverse = norm_apply(attn_out, attention_scale)
    hidden = inputs_local + attn_normed
    mixed_all = gather_rows(hidden.astype(BF16))
    gate_proj = product(mixed_all, gate_cols)
    up_proj = product(mixed_all, up_cols)
    sigmoid_gate = jax.nn.sigmoid(gate_proj)
    active = (gate_proj * sigmoid_gate * up_proj).astype(BF16)
    mlp_out = scatter_rows(
        product(active[:half], down_part), product(active[half:], down_part).astype(BF16)
    )
    mlp_normed, mlp_inverse = norm_apply(mlp_out, feedforward_scale)
    block_output = (hidden + mlp_normed).astype(BF16).reshape(seq_count, local_len, width)

    grad_out = out_grad.reshape(local_len, width).astype(F32)
    mlp_grad, feedforward_part = norm_back(grad_out, mlp_out, mlp_inverse, feedforward_scale)
    mlp_grad_all = gather_rows(mlp_grad.astype(BF16))
    active_grad = right_product(mlp_grad_all, down_part)
    gate_grad = (
        active_grad * up_proj * sigmoid_gate * (1.0 + gate_proj * (1.0 - sigmoid_gate))
    ).astype(BF16)
    up_grad = (active_grad * gate_proj * sigmoid_gate).astype(BF16)
    hidden_grad = grad_out + scatter_rows(
        right_product(gate_grad[:half], gate_cols) + right_product(up_grad[:half], up_cols),
        (
            right_product(gate_grad[half:], gate_cols) + right_product(up_grad[half:], up_cols)
        ).astype(BF16),
    )
    down_term = left_product(active, mlp_grad_all)
    gate_term = left_product(mixed_all, gate_grad)
    up_term = left_product(mixed_all, up_grad)

    attn_grad, attention_part = norm_back(hidden_grad, attn_out, attn_inverse, attention_scale)
    attn_grad_low = attn_grad.astype(BF16)
    context_grad = lax.all_to_all(
        right_product(attn_grad_low, output_full).astype(BF16),
        "sp",
        split_axis=1,
        concat_axis=0,
        tiled=True,
    )
    attn_grad_all = gather_rows(attn_grad_low)
    output_term = left_product(context_own, attn_grad_all)
    query_rot_grad, key_rot_grad, value_grad_low = attention_backward(
        place, query_rot, key_rot, value_low, context_grad, log_total
    )
    (
        query_norm_grad, key_norm_grad, query_dot, key_dot, query_part, key_part,
    ) = rope_backward(
        query_rot_grad, key_rot_grad, query_proj, key_proj, query_inverse, key_inverse,
        query_scale, key_scale, cosine, sine,
    )
    inner = sum_rows(jnp.stack([query_dot[:, 0], key_dot[:, 0]])) / width

    def head_norm_back(incoming, field, inverse, gain, inner_mean):
        scaled = incoming * gain
        return (
            inverse * scaled - field * inverse * inverse * inverse * inner_mean
        ).astype(BF16)

    query_grad_low = head_norm_back(
        query_norm_grad, query_proj, query_inverse, query_scale, inner[0][:, None]
    )
    key_grad_low = head_norm_back(
        key_norm_grad, key_proj, key_inverse, key_scale, inner[1][:, None]
    )

    def input_terms(start):
        span = slice(start, start + half)
        return (
            right_product(query_grad_low[span], query_cols)
            + right_product(key_grad_low[span], key_cols)
            + right_product(value_grad_low[span], value_cols)
        )

    tokens_grad = hidden_grad + scatter_rows(input_terms(0), input_terms(half).astype(BF16))
    tokens_grad = tokens_grad.reshape(seq_count, local_len, width)
    query_term = left_product(inputs_all, query_grad_low)
    key_term = left_product(inputs_all, key_grad_low)
    value_term = left_product(inputs_all, value_grad_low)

    def own_part(term, axis):
        return lax.psum_scatter(
            term.astype(BF16), "fs", scatter_dimension=axis, tiled=True
        ).astype(F32)

    blank = jnp.zeros((width,), F32)
    gain_grads = sum_all(
        jnp.stack(
            [
                lax.dynamic_update_slice_in_dim(blank, query_part[0], column_start, 0),
                lax.dynamic_update_slice_in_dim(blank, key_part[0], column_start, 0),
                attention_part,
                feedforward_part,
            ]
        )
    )
    return (
        block_output,
        tokens_grad,
        own_part(query_term, 0),
        own_part(key_term, 0),
        own_part(value_term, 0),
        own_part(output_term, 1),
        own_part(gate_term, 0),
        own_part(up_term, 0),
        own_part(down_term, 1),
        gain_grads[0],
        gain_grads[1],
        gain_grads[2],
        gain_grads[3],
    )


def inverse_slots(me, count):
    mask = me ^ jnp.arange(count, dtype=jnp.int32)
    return (mask & 1) * (count // 2) + (mask >> 1)


def solution(mesh):
    return jax.shard_map(
        body,
        mesh=mesh,
        in_specs=(
            P("fs", "sp", None),
            P("fs", None),
            P("fs", "sp"),
            P("fs", "sp"),
            P("fs", "sp"),
            P("sp", "fs"),
            P("fs", "sp"),
            P("fs", "sp"),
            P("sp", "fs"),
            P(),
            P(),
            P(),
            P(),
            P("fs", "sp", None),
        ),
        out_specs=(
            P("fs", "sp", None),
            P("fs", "sp", None),
            P("fs", "sp"),
            P("fs", "sp"),
            P("fs", "sp"),
            P("sp", "fs"),
            P("fs", "sp"),
            P("fs", "sp"),
            P("sp", "fs"),
            P(),
            P(),
            P(),
            P(),
        ),
        check_vma=False,
    )
```
